256 devices in a mesh: section: 4 (over x), expert: 64 (over z, y, core).
Axes of the slice: x: 4, y: 4, z: 8, core: 2. Of those that a mesh axis runs over, the one named last changes fastest.
Arguments:
- embedded: bfloat16 [4, 1024, 7168], P('section', 'expert'), may hold values from -6 to 6
- norm_gain: float32 [4, 7168], P('section'), may hold values from 0.1 to 1.9
- gate_proj: bfloat16 [4, 7168, 16384], P('section', None, 'expert'), may hold values from -0.0625 to 0.0625
- up_proj: bfloat16 [4, 7168, 16384], P('section', None, 'expert'), may hold values from -0.0625 to 0.0625
- down_proj: bfloat16 [4, 16384, 7168], P('section', 'expert'), may hold values from -0.125 to 0.125
- expert_ids: int32 [4, 4, 1024, 8], P('section', None, 'expert'), may hold values from 0 to 255, all different within a row; in each aligned block of 16 rows (0 to 15, 16 to 31, ..., all dimensions but the last counted through in order) at most 2 rows name the same one
- route_gates: float32 [4, 4, 1024, 8], P('section', None, 'expert'), may hold values from 0.2 to 2.5
Outputs:
- processed: bfloat16 [4, 1024, 7168], P('section', 'expert')
The draws below stay inside these ranges and needn't reach their ends.
Inputs may be any that keep to these rules, and one draw needn't show every extreme that they name: `expert_ids`: each row names 8 different experts; within one layer and micro-batch no expert is named by more than 2 tokens of an aligned block of 16 tokens.
All inputs are finite; a program needn't handle non-finite values.
Results may differ from the reference program's by a relative error of at most 0.0085.
Values may be sent and summed in bfloat16 or wider, within the bound.
A program may use at most 128 MiB of HBM per device.

```python
import math
import jax
import jax.numpy as jnp
import numpy as np
from jax import lax

D = 7168
ROUTED = 256
TOP = 8
HID_DEV = 256
CAP = 2
TOK_MB = 16
HIDDEN_SIZE = 2048
EXPERTS = 8
LAYERS = 4
MICRO = 4
TOKENS = 1024
N_SECTION = 4
N_EXPERT = 64


def block_levels(rng, shape, shards, least, top_value):
    def one(position, shards_of):
        heights = jax.random.uniform(jax.random.fold_in(jax.random.fold_in(rng, 6), position), (shards_of,), jnp.float32, least / len(shards), top_value / len(shards))
        return jnp.repeat(jnp.exp(heights), shape[position] // shards_of).reshape((-1,) + (1,) * (len(shape) - position - 1))

    loudness = one(*shards[0])
    for cut in shards[1:]:
        loudness = loudness * one(*cut)
    return loudness


def shared_out(key, own, number, rows, amount, top, limit, skew):
    sequence = jax.random.permutation(key, amount)
    packed, common = load_shares(amount, rows * top, limit, skew, True), load_shares(amount, rows * top, limit, skew, False)
    places = jnp.arange(amount)

    def named(tallies, rotation):
        used = int((tallies > 0).sum())
        fixed = max(1, used // 4)
        moved = fixed + (places - fixed + rotation * (used - fixed)) % max(1, amount - fixed)
        return jnp.zeros((amount,), jnp.int32).at[sequence[jnp.where(places < fixed, places, moved)]].set(jnp.asarray(tallies, jnp.int32))

    tallies = jnp.where(number % 4 == 0, named(packed, number // 4), named(common, number - number // 4 - 1))
    mixed = jax.random.permutation(jax.random.fold_in(own, 3), amount)
    donor, receiver = mixed[0:amount // 2 * 2:2], mixed[1:amount // 2 * 2:2]
    slack = jnp.minimum(tallies[donor] - 1, limit - tallies[receiver]) // 2
    slack = jnp.where((donor == sequence[0]) | (receiver == sequence[0]) | (tallies[receiver] == 0), 0, jnp.maximum(slack, 0))
    moved = jax.random.randint(jax.random.fold_in(own, 4), (amount // 2,), 0, 1 << 20) % (slack + 1)
    tallies = tallies.at[donor].add(-moved).at[receiver].add(moved)
    members = jnp.searchsorted(jnp.cumsum(tallies), jnp.arange(rows * top), side="right").astype(jnp.int32)
    table = members.reshape(top, rows).T
    table = table[jax.random.permutation(jax.random.fold_in(own, 1), rows)]
    rotation = jax.random.randint(jax.random.fold_in(own, 2), (rows, 1), 0, top)
    return jnp.take_along_axis(table, (jnp.arange(top)[None, :] + rotation) % top, axis=1)


def load_shares(count, total, reach, skew, full):
    portions = [(1 << 20) // math.isqrt(standing ** skew) + 1 for standing in range(1, count + 1)]
    largest = reach if full else min(reach, max(-(-total // count), total * portions[0] // sum(portions)))
    least = 1 if total - largest >= count - 1 else 0
    given, spare = [largest] + [least] * (count - 1), total - largest - least * (count - 1)
    while spare > 0:
        movable = [i for i in range(1, count) if given[i] < largest] or [i for i in range(1, count) if given[i] < reach]
        pool, budget = sum([portions[i] for i in movable]), spare
        for i in movable:
            more = min(reach - given[i], max(1, budget * portions[i] // pool), spare)
            given[i] = given[i] + more
            spare = spare - more
    return np.array(given)


def normal_values(stream_key, dims, width, most, pieces=(), kind=jnp.bfloat16):
    entries = jax.random.normal(stream_key, dims, jnp.float32) * width
    if len(pieces) > 0:
        entries = block_levels(stream_key, dims, pieces, -0.22, 0.18) * entries
    return jnp.clip(entries, min=-most, max=most).astype(kind)


def setup_inputs(seed: int = 0) -> dict:
    key_list = jax.random.split(jax.random.key(seed), 8)
    embedded = normal_values(key_list[0], (MICRO, TOKENS, D), 1.0, 6.0, ((0, 4), (1, 64)))
    norm_gain = jnp.clip(1.0 + 0.18 * jax.random.normal(key_list[1], (LAYERS, D), jnp.float32), 0.1, 1.9)
    gate_proj = normal_values(key_list[2], (LAYERS, D, EXPERTS * HIDDEN_SIZE), D ** -0.5, 0.0625, ((0, 4), (2, 64)))
    up_proj = normal_values(key_list[3], (LAYERS, D, EXPERTS * HIDDEN_SIZE), D ** -0.5, 0.0625, ((0, 4), (2, 64)))
    down_proj = normal_values(key_list[4], (LAYERS, EXPERTS * HIDDEN_SIZE, D), HIDDEN_SIZE ** -0.5, 0.125, ((0, 4), (1, 64)))
    expert_ids_keys = jax.random.split(jax.random.fold_in(key_list[5], 1), LAYERS * MICRO * TOKENS // TOK_MB)
    expert_ids_turns = jax.random.permutation(jax.random.fold_in(key_list[5], 3), LAYERS * MICRO * TOKENS // TOK_MB)
    expert_ids = jax.vmap(lambda own, number: shared_out(jax.random.fold_in(key_list[5], 2), own, number, TOK_MB, ROUTED, TOP, CAP, 2))(expert_ids_keys, expert_ids_turns).reshape((LAYERS, MICRO, TOKENS, TOP))
    route_gates = jnp.clip(0.2 + 2.3 * jax.random.uniform(key_list[6], (LAYERS, MICRO, TOKENS, TOP), jnp.float32) ** block_levels(key_list[6], (LAYERS, MICRO, TOKENS, TOP), ((0, 4), (2, 64)), -0.2, 0.2), 0.2, 2.5)
    return {"embedded": embedded, "norm_gain": norm_gain, "gate_proj": gate_proj, "up_proj": up_proj, "down_proj": down_proj, "expert_ids": expert_ids, "route_gates": route_gates}


eps_norm = 1e-06

def slot_table(chosen, num_experts):
    expert_range = jnp.arange(num_experts, dtype=jnp.int32)
    matched = (chosen[..., None] == expert_range).astype(jnp.int32)
    hit_table = lax.optimization_barrier(jnp.sum(matched, axis=-2, dtype=jnp.int32))
    earlier = jnp.cumsum(hit_table, axis=-2, dtype=jnp.int32) - hit_table
    slot_index = lax.optimization_barrier(jnp.sum(matched * earlier[..., None, :], axis=-1, dtype=jnp.int32))
    inside = chosen < num_experts
    return (slot_index, inside)

def place_mask(chosen, slot_index, inside, num_experts):
    flat_index = chosen * CAP + slot_index
    target = jnp.arange(num_experts * CAP, dtype=jnp.int32)
    return (flat_index[..., None] == target) & inside[..., None]

def layer_apply(rows, gain_row, gate_mat, up_mat, down_mat, chosen, weights_k):
    group_size = min(8, N_EXPERT)
    num_experts = N_EXPERT // group_size
    width_hidden = group_size * HID_DEV
    rows_float = rows.astype(jnp.float32)
    scale = lax.rsqrt(lax.optimization_barrier(jnp.mean(rows_float * rows_float, axis=-1, keepdims=True)) + eps_norm)
    normed = (rows_float * scale * gain_row.astype(jnp.float32)).astype(jnp.bfloat16)
    blocks = chosen.reshape(N_EXPERT, TOK_MB, TOP)
    slot_index, inside = slot_table(blocks, num_experts)
    placed = place_mask(blocks, slot_index, inside, num_experts)
    mask_any = jnp.any(placed, axis=2).astype(jnp.float32)
    normed_blocks = normed.reshape(N_EXPERT, TOK_MB, D).astype(jnp.float32)
    dispatched = jnp.einsum('ntq,ntd->nqd', mask_any, normed_blocks, precision=lax.Precision.HIGHEST).astype(jnp.bfloat16)
    dispatched = dispatched.reshape(N_EXPERT, num_experts, CAP, D)
    outputs_list = []
    for expert_pos in range(num_experts):
        rows_in = dispatched[:, expert_pos].reshape(N_EXPERT * CAP, D)
        col_start = expert_pos * width_hidden
        gate_val = jnp.dot(rows_in, gate_mat[:, col_start:col_start + width_hidden], preferred_element_type=jnp.float32)
        up_val = jnp.dot(rows_in, up_mat[:, col_start:col_start + width_hidden], preferred_element_type=jnp.float32)
        hidden = (jax.nn.silu(gate_val) * up_val).astype(jnp.bfloat16)
        hidden_parts = hidden.reshape(N_EXPERT * CAP, group_size, HID_DEV).astype(jnp.float32)
        down_parts = down_mat[col_start:col_start + width_hidden].reshape(group_size, HID_DEV, D).astype(jnp.float32)
        partial_value = jnp.einsum('rgi,gid->grd', hidden_parts, down_parts, precision=lax.Precision.HIGHEST).astype(jnp.bfloat16)
        partial_value = lax.optimization_barrier(partial_value)
        summed = lax.optimization_barrier(jnp.sum(partial_value.astype(jnp.float32), axis=0))
        outputs_list.append(summed.reshape(N_EXPERT, CAP, D))
    expert_out = jnp.stack(outputs_list, axis=1).reshape(N_EXPERT, num_experts * CAP, D)
    gates_blocks = weights_k.reshape(N_EXPERT, TOK_MB, TOP)
    weight_table = lax.optimization_barrier(jnp.sum(jnp.where(placed, gates_blocks[..., None], 0.0), axis=2))
    routed_sum = jnp.einsum('ntq,nqd->ntd', weight_table, expert_out, precision=lax.Precision.HIGHEST)
    return (rows_float + routed_sum.reshape(N_EXPERT * TOK_MB, D)).astype(jnp.bfloat16)

def reference(embedded, norm_gain, gate_proj, up_proj, down_proj, expert_ids, route_gates):
    finished = []
    for micro_pos in range(N_SECTION):
        rows = embedded[micro_pos]
        for layer_pos in range(N_SECTION):
            rows = layer_apply(rows, norm_gain[layer_pos], gate_proj[layer_pos], up_proj[layer_pos], down_proj[layer_pos], expert_ids[layer_pos, micro_pos], route_gates[layer_pos, micro_pos])
        finished.append(rows)
    return jnp.stack(finished)
```

```python
import functools

import jax
import jax.numpy as jnp
from jax import lax
from jax.experimental import pallas as pl
from jax.experimental.pallas import tpu as pltpu
from jax.sharding import PartitionSpec as P

MESH = pl.DeviceIdType.MESH
F32 = jnp.float32
BF16 = jnp.bfloat16

D = 7168
J = 8
W = D // J
HID = 256
MB = 4
TOK = 16
CHUNKS = ((0, 512), (512, 384))
EPS = 1e-06
Z_ORDER = (4, 3, 5, 2, 6, 1, 7)


class Refs:
    pass


def scratch_plan():
    dma = pltpu.SemaphoreType.DMA
    plan = [
        ("wg", pltpu.VMEM((D, HID), BF16)),
        ("wu", pltpu.VMEM((D, HID), BF16)),
        ("wd", pltpu.VMEM((HID, D), BF16)),
        ("wsem", dma((3,))),
        ("hb", pltpu.VMEM((128, HID), BF16)),
        ("pm", pltpu.VMEM((MB, 128, 128), BF16)),
        ("cm", pltpu.VMEM((MB + 1, 2, 128, 128), BF16)),
        ("qm", pltpu.VMEM((128, 128), BF16)),
        ("rp", pltpu.VMEM((8, 128), F32)),
        ("rf", pltpu.VMEM((8, 128), F32)),
        ("rp_s", dma),
        ("rf_s", dma((4,))),
        ("rp_r", dma),
        ("rf_r", dma),
        ("xr", pltpu.VMEM((MB + 1, 128, W), BF16)),
        ("xr_r", dma((MB + 1,))),
        ("xi_s", dma),
        ("xc", pltpu.VMEM((MB, 128, W), BF16)),
        ("xc_s", dma((MB,))),
    ]
    for i, (_, w) in enumerate(CHUNKS):
        plan += [
            (f"sz{i}", pltpu.VMEM((MB, 128, w), BF16)),
            (f"rz{i}", pltpu.VMEM((MB, 128, w), BF16)),
            (f"xb{i}", pltpu.VMEM((MB, J, 128, w), BF16)),
            (f"pb{i}", pltpu.VMEM((MB, J, 128, w), BF16)),
            (f"cr{i}", pltpu.VMEM((MB, J, 64, w), BF16)),
            (f"sb{i}", pltpu.VMEM((MB, J, 64, w), BF16)),
            (f"rl{i}", pltpu.VMEM((MB, J // 2, 16, w), BF16)),
            (f"rr{i}", pltpu.VMEM((MB, J // 2, 16, w), BF16)),
            (f"s2{i}", pltpu.VMEM((MB, J, 16, w), BF16)),
            (f"fl{i}", pltpu.VMEM((MB, J, 16, w), BF16)),
            (f"fr{i}", pltpu.VMEM((MB, J, 16, w), BF16)),
            (f"zs{i}", pltpu.VMEM((MB, 128, w), BF16)),
            (f"rt{i}", pltpu.VMEM((MB + 1, 128, w), BF16)),
        ]
        for name in ("szs", "rzr", "ags", "agl", "agr", "afl", "afr", "agc", "rss", "crr", "rlr", "rrr", "flr", "frr", "zss"):
            plan.append((f"{name}{i}", dma((MB,))))
        plan.append((f"rtr{i}", dma((MB + 1,))))
    return plan


PLAN = scratch_plan()


def iotas():
    return (
        lax.broadcasted_iota(jnp.int32, (128, 128), 0),
        lax.broadcasted_iota(jnp.int32, (128, 128), 1),
    )


def dot(a, b):
    return jnp.dot(a, b, preferred_element_type=F32)


def dot_nt(a, b):
    return lax.dot_general(a, b, (((1,), (1,)), ((), ())), preferred_element_type=F32)


def one_hot(cond):
    return jnp.where(cond, 1.0, 0.0).astype(BF16)


def dispatch_matrix(ids_row):
    r, l = iotas()
    named = one_hot(ids_row == (r >> 4).astype(F32))
    same = one_hot((r >> 3) == (l >> 3))
    before = one_hot((r >> 3) < (l >> 3))
    hit = dot(named, same)
    prior = dot(named, before)
    keep = (hit > 0.5) & (prior == (r & 1).astype(F32)) & (((r >> 1) & 7) == (l & 7))
    return one_hot(keep)


def combine_matrices(ids_row, gate_row):
    r, l = iotas()
    hits = jnp.where(ids_row == (r >> 4).astype(F32), 1.0, 0.0)
    named = hits.astype(BF16)
    gated = hits * gate_row
    high = gated.astype(BF16)
    low = (gated - high.astype(F32)).astype(BF16)
    same = one_hot((r >> 3) == (l >> 3))
    before = one_hot((l >> 3) < (r >> 3))
    hit = dot_nt(same, named)
    prior = dot_nt(before, named)
    keep = (hit > 0.5) & (prior == (l & 1).astype(F32)) & (((l >> 1) & 7) == (r & 7))
    return (
        jnp.where(keep, dot_nt(same, high), 0.0).astype(BF16),
        jnp.where(keep, dot_nt(same, low), 0.0).astype(BF16),
    )


def swap_matrix():
    r, l = iotas()
    return one_hot(
        ((r >> 4) == ((l >> 1) & 7)) & (((r >> 1) & 7) == (l >> 4)) & ((r & 1) == (l & 1))
    )


def kernel(x_ref, gain_ref, route_ref, wg_hbm, wu_hbm, wd_hbm, o_ref, *scratch):
    R = Refs()
    for (name, _), ref in zip(PLAN, scratch):
        setattr(R, name, ref)
    get = lambda name, ch: getattr(R, f"{name}{ch}")

    s = lax.axis_index("section")
    ex = lax.axis_index("expert")
    z, y, c = ex // 8, (ex // 2) % 4, ex % 2
    last = s // 3

    def at(z2, y2, c2):
        return (z2 * 4 + y2) * 2 + c2

    up_y, down_y = (s, at(z, (y + 1) % 4, c)), (s, at(z, (y + 3) % 4, c))
    partner = (s, at(z, y, 1 - c))

    def rows(c2, y2):
        return pl.ds(pl.multiple_of((c2 * 4 + y2) * 16, 16), 16)

    def yrows(y2):
        return pl.ds(pl.multiple_of(y2 * 16, 16), 16)

    def half(c2):
        return pl.ds(pl.multiple_of(c2 * 64, 64), 64)

    def send(src, dst, ssem, rsem, dev):
        pltpu.make_async_remote_copy(
            src_ref=src, dst_ref=dst, send_sem=ssem, recv_sem=rsem, device_id=dev, device_id_type=MESH
        ).start()

    def wait(ref, sem):
        pltpu.make_async_copy(ref, ref, sem).wait()

    weights = [
        pltpu.make_async_copy(src, dst, R.wsem.at[i])
        for i, (src, dst) in enumerate(((wg_hbm, R.wg), (wu_hbm, R.wu), (wd_hbm, R.wd)))
    ]
    for copy in weights:
        copy.start()

    barrier = pltpu.get_barrier_semaphore()
    place = s * 8 + z

    def greet(d, carry):
        other = (place + d) % 32
        pl.semaphore_signal(barrier, inc=1, device_id=(other // 8, at(other % 8, y, c)), device_id_type=MESH)
        return carry

    lax.fori_loop(1, 32, greet, 0)
    for dev in (up_y, down_y, partner):
        pl.semaphore_signal(barrier, inc=1, device_id=dev, device_id_type=MESH)

    R.qm[...] = swap_matrix()

    def prepare(m, carry):
        R.pm[m] = dispatch_matrix(route_ref[pl.ds(m, 1), :])
        return carry

    lax.fori_loop(0, MB, prepare, 0)
    pl.semaphore_wait(barrier, 34)

    @pl.when(s < 3)
    def _():
        send(route_ref, R.rp, R.rp_s, R.rp_r, (s + 1, ex))

    @pl.when(s == 3)
    def _():
        for t in range(3):
            send(route_ref, R.rf, R.rf_s.at[t], R.rf_r, (t, ex))
        pltpu.make_async_copy(route_ref, R.rf, R.rf_r).start()

    @pl.when(s > 0)
    def _():
        send(x_ref, R.xr.at[s], R.xi_s, R.xr_r.at[s], (0, ex))

    @pl.when(s == 0)
    def _():
        pltpu.make_async_copy(x_ref, R.xr.at[0], R.xr_r.at[0]).start()

    @pl.when(s > 0)
    def _():
        wait(R.rp, R.rp_r)

        def build(m, carry):
            high, low = combine_matrices(R.rp[pl.ds(m, 1), :], R.rp[pl.ds(m + 4, 1), :])
            R.cm[m, 0] = high
            R.cm[m, 1] = low
            return carry

        lax.fori_loop(0, MB, build, 0)

    def combined(slot, ch, lane, w):
        got = get("rt", ch)[slot]
        added = dot(R.cm[slot, 0], got) + dot(R.cm[slot, 1], got)
        return (R.xr[slot, :, lane : lane + w].astype(F32) + added).astype(BF16)

    def target(m):
        return (1 - last) * (s + 1) + last * m, (1 - last) * m + last * 4

    def stage_a(m):
        wait(R.xr.at[m], R.xr_r.at[m])

        @pl.when(s == 0)
        def _():
            R.xc[m] = R.xr[m]

        @pl.when(s > 0)
        def _():
            for ch, (lane, w) in enumerate(CHUNKS):
                wait(get("rt", ch).at[m], get("rtr", ch).at[m])
                R.xc[m, :, lane : lane + w] = combined(m, ch, lane, w)

        total = jnp.zeros((TOK, J, 1), F32)
        for lane, w in CHUNKS:
            part = R.xc[m, :, lane : lane + w].astype(F32).reshape(TOK, J, w)
            total = total + jnp.sum(part * part, axis=2, keepdims=True)
        scale = lax.rsqrt(jnp.sum(total, axis=1, keepdims=True) * (1.0 / D) + EPS)
        for ch, (lane, w) in enumerate(CHUNKS):
            part = R.xc[m, :, lane : lane + w].astype(F32).reshape(TOK, J, w)
            normed = part * scale * gain_ref[:, lane : lane + w][None]
            normed = normed.reshape(128, w).astype(BF16)
            sz, rz = get("sz", ch), get("rz", ch)
            sz[m] = dot(R.pm[m], normed).astype(BF16)
            mine = pl.ds(pl.multiple_of(z * 16, 16), 16)
            for d in Z_ORDER:
                z2 = (z + d) % 8
                send(
                    sz.at[m, pl.ds(pl.multiple_of(z2 * 16, 16), 16)],
                    rz.at[m, mine],
                    get("szs", ch).at[m],
                    get("rzr", ch).at[m],
                    (s, at(z2, y, c)),
                )
            pltpu.make_async_copy(sz.at[m, mine], rz.at[m, mine], get("rzr", ch).at[m]).start()
        sd, slot = target(m)

        @pl.when(sd != s)
        def _():
            send(R.xc.at[m], R.xr.at[slot], R.xc_s.at[m], R.xr_r.at[slot], (sd, ex))

        @pl.when(sd == s)
        def _():
            pltpu.make_async_copy(R.xc.at[m], R.xr.at[slot], R.xr_r.at[slot]).start()

    def stage_b(m):
        mine = rows(c, y)
        for ch, (_, w) in enumerate(CHUNKS):
            rz, xb = get("rz", ch), get("xb", ch)
            wait(rz.at[m], get("rzr", ch).at[m])
            xb[m, :, mine, :] = dot(R.qm[...], rz[m]).astype(BF16).reshape(J, 16, w)
            block = xb.at[m, :, mine]
            ssem = get("ags", ch).at[m]
            send(block, block, ssem, get("agl", ch).at[m], up_y)
            send(block, block, ssem, get("agr", ch).at[m], down_y)
            send(block, block, ssem, get("agc", ch).at[m], partner)

    def stage_c(m):
        left, right, far = rows(c, (y + 3) % 4), rows(c, (y + 1) % 4), rows(c, (y + 2) % 4)
        low, high = pl.ds(0, J // 2), pl.ds(J // 2, J // 2)
        for ch in range(len(CHUNKS)):
            xb, ssem, csem = get("xb", ch), get("ags", ch).at[m], get("agc", ch).at[m]
            block = xb.at[m, :, left]
            wait(block, get("agl", ch).at[m])
            piece = xb.at[m, low, left]
            send(piece, piece, ssem, get("afl", ch).at[m], up_y)
            send(block, block, ssem, csem, partner)
            block = xb.at[m, :, right]
            wait(block, get("agr", ch).at[m])
            piece = xb.at[m, high, right]
            send(piece, piece, ssem, get("afr", ch).at[m], down_y)
            send(block, block, ssem, csem, partner)
        for ch in range(len(CHUNKS)):
            xb, ssem, csem = get("xb", ch), get("ags", ch).at[m], get("agc", ch).at[m]
            wait(xb.at[m, low, far], get("afl", ch).at[m])
            wait(xb.at[m, high, far], get("afr", ch).at[m])
            block = xb.at[m, :, far]
            send(block, block, ssem, csem, partner)

    def stage_d(m):
        @pl.when(m == 0)
        def _():
            for copy in weights:
                copy.wait()

        gate = jnp.zeros((128, HID), F32)
        up = jnp.zeros((128, HID), F32)
        for ch, (lane, w) in enumerate(CHUNKS):
            xb = get("xb", ch)
            wait(xb.at[m, pl.ds(0, 4)], get("agc", ch).at[m])
            for j in range(J):
                value = xb[m, j]
                gate = gate + dot(value, R.wg[j * W + lane : j * W + lane + w, :])
                up = up + dot(value, R.wu[j * W + lane : j * W + lane + w, :])
        R.hb[...] = (gate * jax.nn.sigmoid(gate) * up).astype(BF16)
        for ch, (lane, w) in enumerate(CHUNKS):
            pb = get("pb", ch)
            for j in range(J):
                pb[m, j] = dot(R.hb[...], R.wd[:, j * W + lane : j * W + lane + w]).astype(BF16)
            send(pb.at[m, :, half(1 - c)], get("cr", ch).at[m], get("rss", ch).at[m], get("crr", ch).at[m], partner)

    def stage_e(m):
        h = J // 2
        low, high = pl.ds(0, h), pl.ds(h, h)
        for ch in range(len(CHUNKS)):
            cr, sb, ssem = get("cr", ch), get("sb", ch), get("rss", ch).at[m]
            wait(cr.at[m], get("crr", ch).at[m])
            for j in range(J):
                own = get("pb", ch)[m, j, half(c), :].astype(F32)
                sb[m, j] = (own + cr[m, j].astype(F32)).astype(BF16)
            far = yrows((y + 2) % 4)
            send(sb.at[m, low, far], get("rl", ch).at[m], ssem, get("rlr", ch).at[m], up_y)
            send(sb.at[m, high, far], get("rr", ch).at[m], ssem, get("rrr", ch).at[m], down_y)
            send(sb.at[m, high, yrows((y + 1) % 4)], get("fl", ch).at[m, high], ssem, get("flr", ch).at[m], up_y)
            send(sb.at[m, low, yrows((y + 3) % 4)], get("fr", ch).at[m, low], ssem, get("frr", ch).at[m], down_y)

    def stage_f(m):
        h = J // 2
        low, high = pl.ds(0, h), pl.ds(h, h)
        for ch in range(len(CHUNKS)):
            sb, s2, ssem = get("sb", ch), get("s2", ch), get("rss", ch).at[m]
            wait(get("rl", ch).at[m], get("rlr", ch).at[m])
            s2[m, low] = (sb[m, low, yrows((y + 1) % 4), :].astype(F32) + get("rl", ch)[m].astype(F32)).astype(BF16)
            send(s2.at[m, low], get("fl", ch).at[m, low], ssem, get("flr", ch).at[m], up_y)
            wait(get("rr", ch).at[m], get("rrr", ch).at[m])
            s2[m, high] = (sb[m, high, yrows((y + 3) % 4), :].astype(F32) + get("rr", ch)[m].astype(F32)).astype(BF16)
            send(s2.at[m, high], get("fr", ch).at[m, high], ssem, get("frr", ch).at[m], down_y)

    def stage_g(m):
        sd, slot = target(m)
        mine = pl.ds(pl.multiple_of(z * 16, 16), 16)
        for ch, (_, w) in enumerate(CHUNKS):
            fl, fr, zs, rt = get("fl", ch), get("fr", ch), get("zs", ch), get("rt", ch)
            wait(fl.at[m], get("flr", ch).at[m])
            wait(fr.at[m], get("frr", ch).at[m])
            total = get("sb", ch)[m, :, yrows(y), :].astype(F32) + fl[m].astype(F32) + fr[m].astype(F32)
            zs[m] = dot(R.qm[...], total.astype(BF16).reshape(128, w)).astype(BF16)
            for d in Z_ORDER:
                z2 = (z + d) % 8
                send(
                    zs.at[m, pl.ds(pl.multiple_of(z2 * 16, 16), 16)],
                    rt.at[slot, mine],
                    get("zss", ch).at[m],
                    get("rtr", ch).at[slot],
                    (sd, at(z2, y, c)),
                )

            @pl.when(sd != s)
            def _():
                send(zs.at[m, mine], rt.at[slot, mine], get("zss", ch).at[m], get("rtr", ch).at[slot], (sd, ex))

            @pl.when(sd == s)
            def _():
                pltpu.make_async_copy(zs.at[m, mine], rt.at[slot, mine], get("rtr", ch).at[slot]).start()

    def turn(i, carry):
        back, front = i >= 1, i < MB

        def on(cond, stage, m):
            pl.when(cond)(functools.partial(stage, m))

        on(back, stage_d, i - 1)
        on(front, stage_a, i)
        on(back, stage_e, i - 1)
        on(front, stage_b, i)
        on(back, stage_f, i - 1)
        on(front, stage_c, i)
        on(back, stage_g, i - 1)
        return carry

    lax.fori_loop(0, MB + 1, turn, 0)

    wait(R.rf, R.rf_r)
    high, low = combine_matrices(R.rf[pl.ds(s, 1), :], R.rf[pl.ds(s + 4, 1), :])
    R.cm[MB, 0] = high
    R.cm[MB, 1] = low
    wait(R.xr.at[MB], R.xr_r.at[MB])
    for ch, (lane, w) in enumerate(CHUNKS):
        wait(get("rt", ch).at[MB], get("rtr", ch).at[MB])
        o_ref[:, lane : lane + w] = combined(MB, ch, lane, w)

    @pl.when(s < 3)
    def _():
        wait(R.rp, R.rp_s)

    @pl.when(s == 3)
    def _():
        for t in range(3):
            wait(R.rf, R.rf_s.at[t])

    @pl.when(s > 0)
    def _():
        wait(x_ref, R.xi_s)

    def drain(m, carry):
        sd, _ = target(m)

        @pl.when(sd != s)
        def _():
            wait(R.xc.at[m], R.xc_s.at[m])

        for ch in range(len(CHUNKS)):
            wait(get("sz", ch).at[m, pl.ds(0, 112)], get("szs", ch).at[m])
            wait(get("xb", ch).at[m, pl.ds(0, 7)], get("ags", ch).at[m])
            wait(get("pb", ch).at[m, pl.ds(0, 7)], get("rss", ch).at[m])

            @pl.when(sd != s)
            def _():
                wait(get("zs", ch).at[m], get("zss", ch).at[m])

            @pl.when(sd == s)
            def _():
                wait(get("zs", ch).at[m, pl.ds(0, 112)], get("zss", ch).at[m])

        return carry

    lax.fori_loop(0, MB, drain, 0)


def shards(embedded, norm_gain, gate_proj, up_proj, down_proj, expert_ids, route_gates):
    rows = embedded.reshape(128, W)
    gain = norm_gain.reshape(J, W)
    route = jnp.concatenate(
        [expert_ids.reshape(MB, 128).astype(F32), route_gates.reshape(MB, 128)], axis=0
    )
    vmem, hbm = pl.BlockSpec(memory_space=pltpu.VMEM), pl.BlockSpec(memory_space=pl.ANY)
    out = pl.pallas_call(
        kernel,
        out_shape=jax.ShapeDtypeStruct((128, W), BF16),
        in_specs=[vmem, vmem, vmem, hbm, hbm, hbm],
        out_specs=vmem,
        scratch_shapes=[shape for _, shape in PLAN],
        compiler_params=pltpu.CompilerParams(
            collective_id=0, has_side_effects=True, vmem_limit_bytes=60 * 1024 * 1024
        ),
        name="expert_sections",
    )(rows, gain, route, gate_proj[0], up_proj[0], down_proj[0])
    return out.reshape(1, TOK, D)


def solution(mesh):
    placed = (
        P("section", "expert", None),
        P("section", None),
        P("section", None, "expert"),
        P("section", None, "expert"),
        P("section", "expert", None),
        P("section", None, "expert", None),
        P("section", None, "expert", None),
    )
    return jax.shard_map(
        shards, mesh=mesh, in_specs=placed, out_specs=P("section", "expert", None), check_vma=False
    )
```

```python
import functools

import jax
import jax.numpy as jnp
from jax import lax
from jax.experimental import pallas as pl
from jax.experimental.pallas import tpu as pltpu
from jax.sharding import PartitionSpec as P

MESH = pl.DeviceIdType.MESH
F32 = jnp.float32
BF16 = jnp.bfloat16

D = 7168
J = 8
W = D // J
HID = 256
MB = 4
TOK = 16
CHUNKS = ((0, 512), (512, 384))
EPS = 1e-06
Z_ORDER = (4, 3, 5, 2, 6, 1, 7)


class Refs:
    pass


def scratch_plan():
    dma = pltpu.SemaphoreType.DMA
    plan = [
        ("wg", pltpu.VMEM((D, HID), BF16)),
        ("wu", pltpu.VMEM((D, HID), BF16)),
        ("wd", pltpu.VMEM((HID, D), BF16)),
        ("wsem", dma((3,))),
        ("hb", pltpu.VMEM((128, HID), BF16)),
        ("pm", pltpu.VMEM((MB, 128, 128), BF16)),
        ("cm", pltpu.VMEM((MB + 1, 2, 128, 128), BF16)),
        ("qm", pltpu.VMEM((128, 128), BF16)),
        ("rpi", pltpu.VMEM((MB, 8, TOK), jnp.int32)),
        ("rpg", pltpu.VMEM((MB, 8, TOK), F32)),
        ("rfi", pltpu.VMEM((8, TOK), jnp.int32)),
        ("rfg", pltpu.VMEM((8, TOK), F32)),
        ("rp_s", dma((2,))),
        ("rf_s", dma((3, 2))),
        ("rp_r", dma((2,))),
        ("rf_r", dma((2,))),
        ("xr", pltpu.VMEM((MB + 1, 128, W), BF16)),
        ("xr_r", dma((MB + 1,))),
        ("xi_s", dma),
        ("xc", pltpu.VMEM((MB, 128, W), BF16)),
        ("xc_s", dma((MB,))),
    ]
    for i, (_, w) in enumerate(CHUNKS):
        plan += [
            (f"sz{i}", pltpu.VMEM((MB, 128, w), BF16)),
            (f"rz{i}", pltpu.VMEM((MB, 128, w), BF16)),
            (f"xb{i}", pltpu.VMEM((MB, J, 128, w), BF16)),
            (f"pb{i}", pltpu.VMEM((MB, J, 128, w), BF16)),
            (f"cr{i}", pltpu.VMEM((MB, J, 64, w), BF16)),
            (f"sb{i}", pltpu.VMEM((MB, J, 64, w), BF16)),
            (f"rl{i}", pltpu.VMEM((MB, J // 2, 16, w), BF16)),
            (f"rr{i}", pltpu.VMEM((MB, J // 2, 16, w), BF16)),
            (f"s2{i}", pltpu.VMEM((MB, J, 16, w), BF16)),
            (f"fl{i}", pltpu.VMEM((MB, J, 16, w), BF16)),
            (f"fr{i}", pltpu.VMEM((MB, J, 16, w), BF16)),
            (f"zs{i}", pltpu.VMEM((MB, 128, w), BF16)),
            (f"rt{i}", pltpu.VMEM((MB + 1, 128, w), BF16)),
        ]
        for name in ("szs", "rzr", "ags", "agl", "agr", "afl", "afr", "agc", "rss", "crr", "rlr", "rrr", "flr", "frr", "zss"):
            plan.append((f"{name}{i}", dma((MB,))))
        plan.append((f"rtr{i}", dma((MB + 1,))))
    return plan


PLAN = scratch_plan()


def iotas():
    return (
        lax.broadcasted_iota(jnp.int32, (128, 128), 0),
        lax.broadcasted_iota(jnp.int32, (128, 128), 1),
    )


def dot(a, b):
    return jnp.dot(a, b, preferred_element_type=F32)


def one_hot(cond):
    return jnp.where(cond, 1.0, 0.0).astype(BF16)


def per_lane(a, pick):
    token = lax.broadcasted_iota(jnp.int32, (TOK, 128), 0)
    lane = lax.broadcasted_iota(jnp.int32, (TOK, 128), 1) & (TOK - 1)
    return dot(a, one_hot(pick(token, lane)))


def chosen(ids, values):
    expert = lax.broadcasted_iota(jnp.int32, (128, TOK), 0) >> 4
    total = jnp.zeros((128, TOK), F32)
    for k in range(8):
        total = total + jnp.where(ids[k : k + 1, :] == expert, values[k : k + 1, :], 0.0)
    return total


def placed(ids):
    r, l = iotas()
    named = chosen(ids, jnp.ones((8, TOK), F32)).astype(BF16)
    hit = per_lane(named, lambda t, lane: t == lane)
    prior = per_lane(named, lambda t, lane: t < lane)
    return (hit > 0.5) & (prior == (r & 1).astype(F32)) & (((r >> 1) & 7) == (l >> 4))


def dispatch_matrix(ids):
    return one_hot(placed(ids))


def combine_matrices(ids, gates):
    keep = placed(ids)
    gated = chosen(ids, gates)
    high = gated.astype(BF16)
    low = (gated - high.astype(F32)).astype(BF16)
    return tuple(
        jnp.where(keep, per_lane(a, lambda t, lane: t == lane), 0.0).T.astype(BF16) for a in (high, low)
    )


def swap_matrix():
    r, l = iotas()
    return one_hot(
        ((r >> 4) == ((l >> 1) & 7)) & (((r >> 1) & 7) == (l >> 4)) & ((r & 1) == (l & 1))
    )


def kernel(x_ref, gain_ref, ids_ref, gates_ref, wg_hbm, wu_hbm, wd_hbm, o_ref, *scratch):
    R = Refs()
    for (name, _), ref in zip(PLAN, scratch):
        setattr(R, name, ref)
    get = lambda name, ch: getattr(R, f"{name}{ch}")

    s = lax.axis_index("section")
    ex = lax.axis_index("expert")
    z, y, c = ex // 8, (ex // 2) % 4, ex % 2
    last = s // 3

    def at(z2, y2, c2):
        return (z2 * 4 + y2) * 2 + c2

    up_y, down_y = (s, at(z, (y + 1) % 4, c)), (s, at(z, (y + 3) % 4, c))
    partner = (s, at(z, y, 1 - c))

    def rows(c2, y2):
        return pl.ds(pl.multiple_of((c2 * 4 + y2) * 16, 16), 16)

    def yrows(y2):
        return pl.ds(pl.multiple_of(y2 * 16, 16), 16)

    def half(c2):
        return pl.ds(pl.multiple_of(c2 * 64, 64), 64)

    def send(src, dst, ssem, rsem, dev):
        pltpu.make_async_remote_copy(
            src_ref=src, dst_ref=dst, send_sem=ssem, recv_sem=rsem, device_id=dev, device_id_type=MESH
        ).start()

    def wait(ref, sem):
        pltpu.make_async_copy(ref, ref, sem).wait()

    weights = [
        pltpu.make_async_copy(src, dst, R.wsem.at[i])
        for i, (src, dst) in enumerate(((wg_hbm, R.wg), (wu_hbm, R.wu), (wd_hbm, R.wd)))
    ]
    for copy in weights:
        copy.start()

    barrier = pltpu.get_barrier_semaphore()
    place = s * 8 + z

    def greet(d, carry):
        other = (place + d) % 32
        pl.semaphore_signal(barrier, inc=1, device_id=(other // 8, at(other % 8, y, c)), device_id_type=MESH)
        return carry

    lax.fori_loop(1, 32, greet, 0)
    for dev in (up_y, down_y, partner):
        pl.semaphore_signal(barrier, inc=1, device_id=dev, device_id_type=MESH)

    R.qm[...] = swap_matrix()

    def prepare(m, carry):
        R.pm[m] = dispatch_matrix(ids_ref[m])
        return carry

    lax.fori_loop(0, MB, prepare, 0)
    pl.semaphore_wait(barrier, 34)

    @pl.when(s < 3)
    def _():
        send(ids_ref, R.rpi, R.rp_s.at[0], R.rp_r.at[0], (s + 1, ex))
        send(gates_ref, R.rpg, R.rp_s.at[1], R.rp_r.at[1], (s + 1, ex))

    @pl.when(s == 3)
    def _():
        for t in range(3):
            send(ids_ref.at[t], R.rfi, R.rf_s.at[t, 0], R.rf_r.at[0], (t, ex))
            send(gates_ref.at[t], R.rfg, R.rf_s.at[t, 1], R.rf_r.at[1], (t, ex))
        pltpu.make_async_copy(ids_ref.at[3], R.rfi, R.rf_r.at[0]).start()
        pltpu.make_async_copy(gates_ref.at[3], R.rfg, R.rf_r.at[1]).start()

    @pl.when(s > 0)
    def _():
        for j in range(J):
            send(x_ref.at[:, pl.ds(j * W, W)], R.xr.at[s, pl.ds(j * TOK, TOK)], R.xi_s, R.xr_r.at[s], (0, ex))

    @pl.when(s == 0)
    def _():
        for j in range(J):
            pltpu.make_async_copy(x_ref.at[:, pl.ds(j * W, W)], R.xr.at[0, pl.ds(j * TOK, TOK)], R.xr_r.at[0]).start()

    @pl.when(s > 0)
    def _():
        wait(R.rpi, R.rp_r.at[0])
        wait(R.rpg, R.rp_r.at[1])

        def build(m, carry):
            high, low = combine_matrices(R.rpi[m], R.rpg[m])
            R.cm[m, 0] = high
            R.cm[m, 1] = low
            return carry

        lax.fori_loop(0, MB, build, 0)

    def combined(slot, ch, lane, w):
        got = get("rt", ch)[slot]
        added = dot(R.cm[slot, 0], got) + dot(R.cm[slot, 1], got)
        return (R.xr[slot, :, lane : lane + w].astype(F32) + added).astype(BF16)

    def target(m):
        return (1 - last) * (s + 1) + last * m, (1 - last) * m + last * 4

    def stage_a(m):
        wait(R.xr.at[m], R.xr_r.at[m])

        @pl.when(s == 0)
        def _():
            R.xc[m] = R.xr[m]

        @pl.when(s > 0)
        def _():
            for ch, (lane, w) in enumerate(CHUNKS):
                wait(get("rt", ch).at[m], get("rtr", ch).at[m])
                R.xc[m, :, lane : lane + w] = combined(m, ch, lane, w)

        total = jnp.zeros((J, TOK, 1), F32)
        for lane, w in CHUNKS:
            part = R.xc[m, :, lane : lane + w].astype(F32).reshape(J, TOK, w)
            total = total + jnp.sum(part * part, axis=2, keepdims=True)
        scale = lax.rsqrt(jnp.sum(total, axis=0) * (1.0 / D) + EPS)
        for ch, (lane, w) in enumerate(CHUNKS):
            pieces = []
            for j in range(J):
                part = R.xc[m, j * TOK : (j + 1) * TOK, lane : lane + w].astype(F32)
                pieces.append((part * scale * gain_ref[:, j * W + lane : j * W + lane + w]).astype(BF16))
            normed = jnp.concatenate(pieces, axis=0)
            sz, rz = get("sz", ch), get("rz", ch)
            sz[m] = dot(R.pm[m], normed).astype(BF16)
            mine = pl.ds(pl.multiple_of(z * 16, 16), 16)
            for d in Z_ORDER:
                z2 = (z + d) % 8
                send(
                    sz.at[m, pl.ds(pl.multiple_of(z2 * 16, 16), 16)],
                    rz.at[m, mine],
                    get("szs", ch).at[m],
                    get("rzr", ch).at[m],
                    (s, at(z2, y, c)),
                )
            pltpu.make_async_copy(sz.at[m, mine], rz.at[m, mine], get("rzr", ch).at[m]).start()
        sd, slot = target(m)

        @pl.when(sd != s)
        def _():
            send(R.xc.at[m], R.xr.at[slot], R.xc_s.at[m], R.xr_r.at[slot], (sd, ex))

        @pl.when(sd == s)
        def _():
            pltpu.make_async_copy(R.xc.at[m], R.xr.at[slot], R.xr_r.at[slot]).start()

    def stage_b(m):
        mine = rows(c, y)
        for ch, (_, w) in enumerate(CHUNKS):
            rz, xb = get("rz", ch), get("xb", ch)
            wait(rz.at[m], get("rzr", ch).at[m])
            xb[m, :, mine, :] = dot(R.qm[...], rz[m]).astype(BF16).reshape(J, 16, w)
            block = xb.at[m, :, mine]
            ssem = get("ags", ch).at[m]
            send(block, block, ssem, get("agl", ch).at[m], up_y)
            send(block, block, ssem, get("agr", ch).at[m], down_y)
            send(block, block, ssem, get("agc", ch).at[m], partner)

    def stage_c(m):
        left, right, far = rows(c, (y + 3) % 4), rows(c, (y + 1) % 4), rows(c, (y + 2) % 4)
        low, high = pl.ds(0, J // 2), pl.ds(J // 2, J // 2)
        for ch in range(len(CHUNKS)):
            xb, ssem, csem = get("xb", ch), get("ags", ch).at[m], get("agc", ch).at[m]
            block = xb.at[m, :, left]
            wait(block, get("agl", ch).at[m])
            piece = xb.at[m, low, left]
            send(piece, piece, ssem, get("afl", ch).at[m], up_y)
            send(block, block, ssem, csem, partner)
            block = xb.at[m, :, right]
            wait(block, get("agr", ch).at[m])
            piece = xb.at[m, high, right]
            send(piece, piece, ssem, get("afr", ch).at[m], down_y)
            send(block, block, ssem, csem, partner)
        for ch in range(len(CHUNKS)):
            xb, ssem, csem = get("xb", ch), get("ags", ch).at[m], get("agc", ch).at[m]
            wait(xb.at[m, low, far], get("afl", ch).at[m])
            wait(xb.at[m, high, far], get("afr", ch).at[m])
            block = xb.at[m, :, far]
            send(block, block, ssem, csem, partner)

    def stage_d(m):
        @pl.when(m == 0)
        def _():
            for copy in weights:
                copy.wait()

        gate = jnp.zeros((128, HID), F32)
        up = jnp.zeros((128, HID), F32)
        for ch, (lane, w) in enumerate(CHUNKS):
            xb = get("xb", ch)
            wait(xb.at[m, pl.ds(0, 4)], get("agc", ch).at[m])
            for j in range(J):
                value = xb[m, j]
                gate = gate + dot(value, R.wg[j * W + lane : j * W + lane + w, :])
                up = up + dot(value, R.wu[j * W + lane : j * W + lane + w, :])
        R.hb[...] = (gate * jax.nn.sigmoid(gate) * up).astype(BF16)
        for ch, (lane, w) in enumerate(CHUNKS):
            pb = get("pb", ch)
            for j in range(J):
                pb[m, j] = dot(R.hb[...], R.wd[:, j * W + lane : j * W + lane + w]).astype(BF16)
            send(pb.at[m, :, half(1 - c)], get("cr", ch).at[m], get("rss", ch).at[m], get("crr", ch).at[m], partner)

    def stage_e(m):
        h = J // 2
        low, high = pl.ds(0, h), pl.ds(h, h)
        for ch in range(len(CHUNKS)):
            cr, sb, ssem = get("cr", ch), get("sb", ch), get("rss", ch).at[m]
            wait(cr.at[m], get("crr", ch).at[m])
            for j in range(J):
                own = get("pb", ch)[m, j, half(c), :].astype(F32)
                sb[m, j] = (own + cr[m, j].astype(F32)).astype(BF16)
            far = yrows((y + 2) % 4)
            send(sb.at[m, low, far], get("rl", ch).at[m], ssem, get("rlr", ch).at[m], up_y)
            send(sb.at[m, high, far], get("rr", ch).at[m], ssem, get("rrr", ch).at[m], down_y)
            send(sb.at[m, high, yrows((y + 1) % 4)], get("fl", ch).at[m, high], ssem, get("flr", ch).at[m], up_y)
            send(sb.at[m, low, yrows((y + 3) % 4)], get("fr", ch).at[m, low], ssem, get("frr", ch).at[m], down_y)

    def stage_f(m):
        h = J // 2
        low, high = pl.ds(0, h), pl.ds(h, h)
        for ch in range(len(CHUNKS)):
            sb, s2, ssem = get("sb", ch), get("s2", ch), get("rss", ch).at[m]
            wait(get("rl", ch).at[m], get("rlr", ch).at[m])
            s2[m, low] = (sb[m, low, yrows((y + 1) % 4), :].astype(F32) + get("rl", ch)[m].astype(F32)).astype(BF16)
            send(s2.at[m, low], get("fl", ch).at[m, low], ssem, get("flr", ch).at[m], up_y)
            wait(get("rr", ch).at[m], get("rrr", ch).at[m])
            s2[m, high] = (sb[m, high, yrows((y + 3) % 4), :].astype(F32) + get("rr", ch)[m].astype(F32)).astype(BF16)
            send(s2.at[m, high], get("fr", ch).at[m, high], ssem, get("frr", ch).at[m], down_y)

    def stage_g(m):
        sd, slot = target(m)
        mine = pl.ds(pl.multiple_of(z * 16, 16), 16)
        for ch, (_, w) in enumerate(CHUNKS):
            fl, fr, zs, rt = get("fl", ch), get("fr", ch), get("zs", ch), get("rt", ch)
            wait(fl.at[m], get("flr", ch).at[m])
            wait(fr.at[m], get("frr", ch).at[m])
            total = get("sb", ch)[m, :, yrows(y), :].astype(F32) + fl[m].astype(F32) + fr[m].astype(F32)
            zs[m] = dot(R.qm[...], total.astype(BF16).reshape(128, w)).astype(BF16)
            for d in Z_ORDER:
                z2 = (z + d) % 8
                send(
                    zs.at[m, pl.ds(pl.multiple_of(z2 * 16, 16), 16)],
                    rt.at[slot, mine],
                    get("zss", ch).at[m],
                    get("rtr", ch).at[slot],
                    (sd, at(z2, y, c)),
                )

            @pl.when(sd != s)
            def _():
                send(zs.at[m, mine], rt.at[slot, mine], get("zss", ch).at[m], get("rtr", ch).at[slot], (sd, ex))

            @pl.when(sd == s)
            def _():
                pltpu.make_async_copy(zs.at[m, mine], rt.at[slot, mine], get("rtr", ch).at[slot]).start()

    def turn(i, carry):
        back, front = i >= 1, i < MB

        def on(cond, stage, m):
            pl.when(cond)(functools.partial(stage, m))

        on(back, stage_d, i - 1)
        on(front, stage_a, i)
        on(back, stage_e, i - 1)
        on(front, stage_b, i)
        on(back, stage_f, i - 1)
        on(front, stage_c, i)
        on(back, stage_g, i - 1)
        return carry

    lax.fori_loop(0, MB + 1, turn, 0)

    wait(R.rfi, R.rf_r.at[0])
    wait(R.rfg, R.rf_r.at[1])
    high, low = combine_matrices(R.rfi[...], R.rfg[...])
    R.cm[MB, 0] = high
    R.cm[MB, 1] = low
    wait(R.xr.at[MB], R.xr_r.at[MB])
    for ch, (lane, w) in enumerate(CHUNKS):
        wait(get("rt", ch).at[MB], get("rtr", ch).at[MB])
        value = combined(MB, ch, lane, w)
        for j in range(J):
            o_ref[:, j * W + lane : j * W + lane + w] = value[j * TOK : (j + 1) * TOK]

    @pl.when(s < 3)
    def _():
        wait(R.rpi, R.rp_s.at[0])
        wait(R.rpg, R.rp_s.at[1])

    @pl.when(s == 3)
    def _():
        for t in range(3):
            wait(R.rfi, R.rf_s.at[t, 0])
            wait(R.rfg, R.rf_s.at[t, 1])

    @pl.when(s > 0)
    def _():
        wait(x_ref, R.xi_s)

    def drain(m, carry):
        sd, _ = target(m)

        @pl.when(sd != s)
        def _():
            wait(R.xc.at[m], R.xc_s.at[m])

        for ch in range(len(CHUNKS)):
            wait(get("sz", ch).at[m, pl.ds(0, 112)], get("szs", ch).at[m])
            wait(get("xb", ch).at[m, pl.ds(0, 7)], get("ags", ch).at[m])
            wait(get("pb", ch).at[m, pl.ds(0, 7)], get("rss", ch).at[m])

            @pl.when(sd != s)
            def _():
                wait(get("zs", ch).at[m], get("zss", ch).at[m])

            @pl.when(sd == s)
            def _():
                wait(get("zs", ch).at[m, pl.ds(0, 112)], get("zss", ch).at[m])

        return carry

    lax.fori_loop(0, MB, drain, 0)


def shards(embedded, norm_gain, gate_proj, up_proj, down_proj, expert_ids, route_gates):
    vmem, hbm = pl.BlockSpec(memory_space=pltpu.VMEM), pl.BlockSpec(memory_space=pl.ANY)
    out = pl.pallas_call(
        kernel,
        out_shape=jax.ShapeDtypeStruct((TOK, D), BF16),
        in_specs=[vmem, vmem, vmem, vmem, hbm, hbm, hbm],
        out_specs=vmem,
        scratch_shapes=[shape for _, shape in PLAN],
        compiler_params=pltpu.CompilerParams(
            collective_id=0, has_side_effects=True, vmem_limit_bytes=60 * 1024 * 1024
        ),
        name="expert_sections",
    )(embedded[0], norm_gain, expert_ids[0].swapaxes(1, 2), route_gates[0].swapaxes(1, 2), gate_proj[0], up_proj[0], down_proj[0])
    return out[None]


def solution(mesh):
    specs = (
        P("section", "expert", None),
        P("section", None),
        P("section", None, "expert"),
        P("section", None, "expert"),
        P("section", "expert", None),
        P("section", None, "expert", None),
        P("section", None, "expert", None),
    )
    return jax.shard_map(
        shards, mesh=mesh, in_specs=specs, out_specs=P("section", "expert", None), check_vma=False
    )
```

```python
import functools

import jax
import jax.numpy as jnp
from jax import lax
from jax.experimental import pallas as pl
from jax.experimental.pallas import tpu as pltpu
from jax.sharding import PartitionSpec as P

MESH = pl.DeviceIdType.MESH
F32 = jnp.float32
BF16 = jnp.bfloat16

D = 7168
J = 8
W = D // J
HID = 256
MB = 4
TOK = 16
CHUNKS = ((0, 512), (512, 384))
EPS = 1e-06
Z_ORDER = (4, 3, 5, 2, 6, 1, 7)


class Refs:
    pass


def scratch_plan():
    dma = pltpu.SemaphoreType.DMA
    plan = [
        ("wg", pltpu.VMEM((D, HID), BF16)),
        ("wu", pltpu.VMEM((D, HID), BF16)),
        ("wd", pltpu.VMEM((HID, D), BF16)),
        ("wsem", dma((3,))),
        ("hb", pltpu.VMEM((128, HID), BF16)),
        ("pm", pltpu.VMEM((MB, 128, 128), BF16)),
        ("cm", pltpu.VMEM((MB + 1, 2, 128, 128), BF16)),
        ("qm", pltpu.VMEM((128, 128), BF16)),
        ("rpi", pltpu.VMEM((MB, 8, TOK), jnp.int32)),
        ("rpg", pltpu.VMEM((MB, 8, TOK), F32)),
        ("rfi", pltpu.VMEM((8, TOK), jnp.int32)),
        ("rfg", pltpu.VMEM((8, TOK), F32)),
        ("rp_s", dma((2,))),
        ("rf_s", dma((3, 2))),
        ("rp_r", dma((2,))),
        ("rf_r", dma((2,))),
        ("xr", pltpu.VMEM((MB + 1, 128, W), BF16)),
        ("xr_r", dma((MB + 1,))),
        ("xi_s", dma),
        ("xc", pltpu.VMEM((MB, 128, W), BF16)),
        ("xc_s", dma((MB,))),
    ]
    for i, (_, w) in enumerate(CHUNKS):
        plan += [
            (f"sz{i}", pltpu.VMEM((MB, 128, w), BF16)),
            (f"rz{i}", pltpu.VMEM((MB, 128, w), BF16)),
            (f"xb{i}", pltpu.VMEM((MB, J, 128, w), BF16)),
            (f"pb{i}", pltpu.VMEM((MB, J, 128, w), BF16)),
            (f"cr{i}", pltpu.VMEM((MB, J, 64, w), BF16)),
            (f"sb{i}", pltpu.VMEM((MB, J, 64, w), BF16)),
            (f"rl{i}", pltpu.VMEM((MB, J // 2, 16, w), BF16)),
            (f"rr{i}", pltpu.VMEM((MB, J // 2, 16, w), BF16)),
            (f"s2{i}", pltpu.VMEM((MB, J, 16, w), BF16)),
            (f"fl{i}", pltpu.VMEM((MB, J, 16, w), BF16)),
            (f"fr{i}", pltpu.VMEM((MB, J, 16, w), BF16)),
            (f"zs{i}", pltpu.VMEM((MB, 128, w), BF16)),
            (f"rt{i}", pltpu.VMEM((MB + 1, 128, w), BF16)),
        ]
        for name in ("szs", "rzr", "ags", "agl", "agr", "afl", "afr", "agc", "rss", "crr", "rlr", "rrr", "flr", "frr", "zss"):
            plan.append((f"{name}{i}", dma((MB,))))
        plan.append((f"rtr{i}", dma((MB + 1,))))
    return plan


PLAN = scratch_plan()


def iotas():
    return (
        lax.broadcasted_iota(jnp.int32, (128, 128), 0),
        lax.broadcasted_iota(jnp.int32, (128, 128), 1),
    )


def dot(a, b):
    return jnp.dot(a, b, preferred_element_type=F32)


def one_hot(cond):
    return jnp.where(cond, 1.0, 0.0).astype(BF16)


def per_lane(a, pick):
    token = lax.broadcasted_iota(jnp.int32, (TOK, 128), 0)
    lane = lax.broadcasted_iota(jnp.int32, (TOK, 128), 1) & (TOK - 1)
    return dot(a, one_hot(pick(token, lane)))


def chosen(ids, values):
    expert = lax.broadcasted_iota(jnp.int32, (128, TOK), 0) >> 4
    total = jnp.zeros((128, TOK), F32)
    for k in range(8):
        total = total + jnp.where(ids[k : k + 1, :] == expert, values[k : k + 1, :], 0.0)
    return total


def placed(ids):
    r, l = iotas()
    named = chosen(ids, jnp.ones((8, TOK), F32)).astype(BF16)
    hit = per_lane(named, lambda t, lane: t == lane)
    prior = per_lane(named, lambda t, lane: t < lane)
    return (hit > 0.5) & (prior == (r & 1).astype(F32)) & (((r >> 1) & 7) == (l >> 4))


def dispatch_matrix(ids):
    return one_hot(placed(ids))


def combine_matrices(ids, gates):
    keep = placed(ids)
    gated = chosen(ids, gates)
    high = gated.astype(BF16)
    low = (gated - high.astype(F32)).astype(BF16)
    return tuple(
        jnp.where(keep, per_lane(a, lambda t, lane: t == lane), 0.0).T.astype(BF16) for a in (high, low)
    )


def swap_matrix():
    r, l = iotas()
    return one_hot(
        ((r >> 4) == ((l >> 1) & 7)) & (((r >> 1) & 7) == (l >> 4)) & ((r & 1) == (l & 1))
    )


def kernel(x_ref, gain_ref, ids_ref, gates_ref, wg_hbm, wu_hbm, wd_hbm, o_ref, *scratch):
    R = Refs()
    for (name, _), ref in zip(PLAN, scratch):
        setattr(R, name, ref)
    get = lambda name, ch: getattr(R, f"{name}{ch}")

    s = lax.axis_index("section")
    ex = lax.axis_index("expert")
    z, y, c = ex // 8, (ex // 2) % 4, ex % 2
    last = s // 3

    def at(z2, y2, c2):
        return (z2 * 4 + y2) * 2 + c2

    up_y, down_y = (s, at(z, (y + 1) % 4, c)), (s, at(z, (y + 3) % 4, c))
    partner = (s, at(z, y, 1 - c))

    def rows(c2, y2):
        return pl.ds(pl.multiple_of((c2 * 4 + y2) * 16, 16), 16)

    def yrows(y2):
        return pl.ds(pl.multiple_of(y2 * 16, 16), 16)

    def half(c2):
        return pl.ds(pl.multiple_of(c2 * 64, 64), 64)

    def send(src, dst, ssem, rsem, dev):
        pltpu.make_async_remote_copy(
            src_ref=src, dst_ref=dst, send_sem=ssem, recv_sem=rsem, device_id=dev, device_id_type=MESH
        ).start()

    def wait(ref, sem):
        pltpu.make_async_copy(ref, ref, sem).wait()

    weights = [
        pltpu.make_async_copy(src, dst, R.wsem.at[i])
        for i, (src, dst) in enumerate(((wg_hbm, R.wg), (wu_hbm, R.wu), (wd_hbm, R.wd)))
    ]
    for copy in weights:
        copy.start()

    barrier = pltpu.get_barrier_semaphore()
    place = s * 8 + z

    def greet(d, carry):
        other = (place + d) % 32
        pl.semaphore_signal(barrier, inc=1, device_id=(other // 8, at(other % 8, y, c)), device_id_type=MESH)
        return carry

    lax.fori_loop(1, 32, greet, 0)
    for dev in (up_y, down_y, partner):
        pl.semaphore_signal(barrier, inc=1, device_id=dev, device_id_type=MESH)

    R.qm[...] = swap_matrix()

    def prepare(m, carry):
        R.pm[m] = dispatch_matrix(ids_ref[m])
        return carry

    lax.fori_loop(0, MB, prepare, 0)
    pl.semaphore_wait(barrier, 34)

    @pl.when(s < 3)
    def _():
        send(ids_ref, R.rpi, R.rp_s.at[0], R.rp_r.at[0], (s + 1, ex))
        send(gates_ref, R.rpg, R.rp_s.at[1], R.rp_r.at[1], (s + 1, ex))

    @pl.when(s == 3)
    def _():
        for t in range(3):
            send(ids_ref.at[t], R.rfi, R.rf_s.at[t, 0], R.rf_r.at[0], (t, ex))
            send(gates_ref.at[t], R.rfg, R.rf_s.at[t, 1], R.rf_r.at[1], (t, ex))
        pltpu.make_async_copy(ids_ref.at[3], R.rfi, R.rf_r.at[0]).start()
        pltpu.make_async_copy(gates_ref.at[3], R.rfg, R.rf_r.at[1]).start()

    @pl.when(s > 0)
    def _():
        for j in range(J):
            send(x_ref.at[:, pl.ds(j * W, W)], R.xr.at[s, pl.ds(j * TOK, TOK)], R.xi_s, R.xr_r.at[s], (0, ex))

    @pl.when(s == 0)
    def _():
        for j in range(J):
            pltpu.make_async_copy(x_ref.at[:, pl.ds(j * W, W)], R.xr.at[0, pl.ds(j * TOK, TOK)], R.xr_r.at[0]).start()

    @pl.when(s > 0)
    def _():
        wait(R.rpi, R.rp_r.at[0])
        wait(R.rpg, R.rp_r.at[1])

        def build(m, carry):
            high, low = combine_matrices(R.rpi[m], R.rpg[m])
            R.cm[m, 0] = high
            R.cm[m, 1] = low
            return carry

        lax.fori_loop(0, MB, build, 0)

    def combined(slot, ch, lane, w):
        got = get("rt", ch)[slot]
        added = dot(R.cm[slot, 0], got) + dot(R.cm[slot, 1], got)
        return (R.xr[slot, :, lane : lane + w].astype(F32) + added).astype(BF16)

    def target(m):
        return (1 - last) * (s + 1) + last * m, (1 - last) * m + last * 4

    def stage_a(m):
        wait(R.xr.at[m], R.xr_r.at[m])

        @pl.when(s == 0)
        def _():
            R.xc[m] = R.xr[m]

        @pl.when(s > 0)
        def _():
            for ch, (lane, w) in enumerate(CHUNKS):
                wait(get("rt", ch).at[m], get("rtr", ch).at[m])
                R.xc[m, :, lane : lane + w] = combined(m, ch, lane, w)

        total = jnp.zeros((J, TOK, 1), F32)
        for lane, w in CHUNKS:
            part = R.xc[m, :, lane : lane + w].astype(F32).reshape(J, TOK, w)
            total = total + jnp.sum(part * part, axis=2, keepdims=True)
        scale = lax.rsqrt(jnp.sum(total, axis=0) * (1.0 / D) + EPS)
        for ch, (lane, w) in enumerate(CHUNKS):
            pieces = []
            for j in range(J):
                part = R.xc[m, j * TOK : (j + 1) * TOK, lane : lane + w].astype(F32)
                pieces.append((part * scale * gain_ref[:, j * W + lane : j * W + lane + w]).astype(BF16))
            normed = jnp.concatenate(pieces, axis=0)
            sz, rz = get("sz", ch), get("rz", ch)
            sz[m] = dot(R.pm[m], normed).astype(BF16)
            mine = pl.ds(pl.multiple_of(z * 16, 16), 16)
            for d in Z_ORDER:
                z2 = (z + d) % 8
                send(
                    sz.at[m, pl.ds(pl.multiple_of(z2 * 16, 16), 16)],
                    rz.at[m, mine],
                    get("szs", ch).at[m],
                    get("rzr", ch).at[m],
                    (s, at(z2, y, c)),
                )
            pltpu.make_async_copy(sz.at[m, mine], rz.at[m, mine], get("rzr", ch).at[m]).start()
        sd, slot = target(m)

        @pl.when(sd != s)
        def _():
            send(R.xc.at[m], R.xr.at[slot], R.xc_s.at[m], R.xr_r.at[slot], (sd, ex))

        @pl.when(sd == s)
        def _():
            pltpu.make_async_copy(R.xc.at[m], R.xr.at[slot], R.xr_r.at[slot]).start()

    def stage_b(m):
        mine = rows(c, y)
        for ch, (_, w) in enumerate(CHUNKS):
            rz, xb = get("rz", ch), get("xb", ch)
            wait(rz.at[m], get("rzr", ch).at[m])
            xb[m, :, mine, :] = dot(R.qm[...], rz[m]).astype(BF16).reshape(J, 16, w)
            block = xb.at[m, :, mine]
            ssem = get("ags", ch).at[m]
            send(block, block, ssem, get("agl", ch).at[m], up_y)
            send(block, block, ssem, get("agr", ch).at[m], down_y)
            send(block, block, ssem, get("agc", ch).at[m], partner)

    def stage_c(m):
        left, right, far = rows(c, (y + 3) % 4), rows(c, (y + 1) % 4), rows(c, (y + 2) % 4)
        low, high = pl.ds(0, J // 2), pl.ds(J // 2, J // 2)
        for ch in range(len(CHUNKS)):
            xb, ssem, csem = get("xb", ch), get("ags", ch).at[m], get("agc", ch).at[m]
            block = xb.at[m, :, left]
            wait(block, get("agl", ch).at[m])
            piece = xb.at[m, low, left]
            send(piece, piece, ssem, get("afl", ch).at[m], up_y)
            send(block, block, ssem, csem, partner)
            block = xb.at[m, :, right]
            wait(block, get("agr", ch).at[m])
            piece = xb.at[m, high, right]
            send(piece, piece, ssem, get("afr", ch).at[m], down_y)
            send(block, block, ssem, csem, partner)
        for ch in range(len(CHUNKS)):
            xb, ssem, csem = get("xb", ch), get("ags", ch).at[m], get("agc", ch).at[m]
            wait(xb.at[m, low, far], get("afl", ch).at[m])
            wait(xb.at[m, high, far], get("afr", ch).at[m])
            block = xb.at[m, :, far]
            send(block, block, ssem, csem, partner)

    def stage_d(m):
        @pl.when(m == 0)
        def _():
            for copy in weights:
                copy.wait()

        gate = jnp.zeros((128, HID), F32)
        up = jnp.zeros((128, HID), F32)
        for ch, (lane, w) in enumerate(CHUNKS):
            xb = get("xb", ch)
            wait(xb.at[m, pl.ds(0, 4)], get("agc", ch).at[m])
            for j in range(J):
                value = xb[m, j]
                gate = gate + dot(value, R.wg[j * W + lane : j * W + lane + w, :])
                up = up + dot(value, R.wu[j * W + lane : j * W + lane + w, :])
        R.hb[...] = (gate * jax.nn.sigmoid(gate) * up).astype(BF16)
        for ch, (lane, w) in enumerate(CHUNKS):
            pb = get("pb", ch)
            for j in range(J):
                pb[m, j] = dot(R.hb[...], R.wd[:, j * W + lane : j * W + lane + w]).astype(BF16)
            send(pb.at[m, :, half(1 - c)], get("cr", ch).at[m], get("rss", ch).at[m], get("crr", ch).at[m], partner)

    def stage_e(m):
        h = J // 2
        low, high = pl.ds(0, h), pl.ds(h, h)
        for ch in range(len(CHUNKS)):
            cr, sb, ssem = get("cr", ch), get("sb", ch), get("rss", ch).at[m]
            wait(cr.at[m], get("crr", ch).at[m])
            for j in range(J):
                own = get("pb", ch)[m, j, half(c), :].astype(F32)
                sb[m, j] = (own + cr[m, j].astype(F32)).astype(BF16)
            far = yrows((y + 2) % 4)
            send(sb.at[m, low, far], get("rl", ch).at[m], ssem, get("rlr", ch).at[m], up_y)
            send(sb.at[m, high, far], get("rr", ch).at[m], ssem, get("rrr", ch).at[m], down_y)
            send(sb.at[m, high, yrows((y + 1) % 4)], get("fl", ch).at[m, high], ssem, get("flr", ch).at[m], up_y)
            send(sb.at[m, low, yrows((y + 3) % 4)], get("fr", ch).at[m, low], ssem, get("frr", ch).at[m], down_y)

    def stage_f(m):
        h = J // 2
        low, high = pl.ds(0, h), pl.ds(h, h)
        for ch in range(len(CHUNKS)):
            sb, s2, ssem = get("sb", ch), get("s2", ch), get("rss", ch).at[m]
            wait(get("rl", ch).at[m], get("rlr", ch).at[m])
            s2[m, low] = (sb[m, low, yrows((y + 1) % 4), :].astype(F32) + get("rl", ch)[m].astype(F32)).astype(BF16)
            send(s2.at[m, low], get("fl", ch).at[m, low], ssem, get("flr", ch).at[m], up_y)
            wait(get("rr", ch).at[m], get("rrr", ch).at[m])
            s2[m, high] = (sb[m, high, yrows((y + 3) % 4), :].astype(F32) + get("rr", ch)[m].astype(F32)).astype(BF16)
            send(s2.at[m, high], get("fr", ch).at[m, high], ssem, get("frr", ch).at[m], down_y)

    def stage_g(m):
        sd, slot = target(m)
        mine = pl.ds(pl.multiple_of(z * 16, 16), 16)
        for ch, (_, w) in enumerate(CHUNKS):
            fl, fr, zs, rt = get("fl", ch), get("fr", ch), get("zs", ch), get("rt", ch)
            wait(fl.at[m], get("flr", ch).at[m])
            wait(fr.at[m], get("frr", ch).at[m])
            total = get("sb", ch)[m, :, yrows(y), :].astype(F32) + fl[m].astype(F32) + fr[m].astype(F32)
            zs[m] = dot(R.qm[...], total.astype(BF16).reshape(128, w)).astype(BF16)
            for d in Z_ORDER:
                z2 = (z + d) % 8
                send(
                    zs.at[m, pl.ds(pl.multiple_of(z2 * 16, 16), 16)],
                    rt.at[slot, mine],
                    get("zss", ch).at[m],
                    get("rtr", ch).at[slot],
                    (sd, at(z2, y, c)),
                )

            @pl.when(sd != s)
            def _():
                send(zs.at[m, mine], rt.at[slot, mine], get("zss", ch).at[m], get("rtr", ch).at[slot], (sd, ex))

            @pl.when(sd == s)
            def _():
                pltpu.make_async_copy(zs.at[m, mine], rt.at[slot, mine], get("rtr", ch).at[slot]).start()

    def turn(i, carry):
        back, front = i >= 1, i < MB

        def on(cond, stage, m):
            pl.when(cond)(functools.partial(stage, m))

        on(back, stage_d, i - 1)
        on(back, stage_e, i - 1)
        on(front, stage_a, i)
        on(back, stage_f, i - 1)
        on(front, stage_b, i)
        on(back, stage_g, i - 1)
        on(front, stage_c, i)
        return carry

    lax.fori_loop(0, MB + 1, turn, 0)

    wait(R.rfi, R.rf_r.at[0])
    wait(R.rfg, R.rf_r.at[1])
    high, low = combine_matrices(R.rfi[...], R.rfg[...])
    R.cm[MB, 0] = high
    R.cm[MB, 1] = low
    wait(R.xr.at[MB], R.xr_r.at[MB])
    for ch, (lane, w) in enumerate(CHUNKS):
        wait(get("rt", ch).at[MB], get("rtr", ch).at[MB])
        value = combined(MB, ch, lane, w)
        for j in range(J):
            o_ref[:, j * W + lane : j * W + lane + w] = value[j * TOK : (j + 1) * TOK]

    @pl.when(s < 3)
    def _():
        wait(R.rpi, R.rp_s.at[0])
        wait(R.rpg, R.rp_s.at[1])

    @pl.when(s == 3)
    def _():
        for t in range(3):
            wait(R.rfi, R.rf_s.at[t, 0])
            wait(R.rfg, R.rf_s.at[t, 1])

    @pl.when(s > 0)
    def _():
        wait(x_ref, R.xi_s)

    def drain(m, carry):
        sd, _ = target(m)

        @pl.when(sd != s)
        def _():
            wait(R.xc.at[m], R.xc_s.at[m])

        for ch in range(len(CHUNKS)):
            wait(get("sz", ch).at[m, pl.ds(0, 112)], get("szs", ch).at[m])
            wait(get("xb", ch).at[m, pl.ds(0, 7)], get("ags", ch).at[m])
            wait(get("pb", ch).at[m, pl.ds(0, 7)], get("rss", ch).at[m])

            @pl.when(sd != s)
            def _():
                wait(get("zs", ch).at[m], get("zss", ch).at[m])

            @pl.when(sd == s)
            def _():
                wait(get("zs", ch).at[m, pl.ds(0, 112)], get("zss", ch).at[m])

        return carry

    lax.fori_loop(0, MB, drain, 0)


def shards(embedded, norm_gain, gate_proj, up_proj, down_proj, expert_ids, route_gates):
    vmem, hbm = pl.BlockSpec(memory_space=pltpu.VMEM), pl.BlockSpec(memory_space=pl.ANY)
    out = pl.pallas_call(
        kernel,
        out_shape=jax.ShapeDtypeStruct((TOK, D), BF16),
        in_specs=[vmem, vmem, vmem, vmem, hbm, hbm, hbm],
        out_specs=vmem,
        scratch_shapes=[shape for _, shape in PLAN],
        compiler_params=pltpu.CompilerParams(
            collective_id=0, has_side_effects=True, vmem_limit_bytes=60 * 1024 * 1024
        ),
        name="expert_sections",
    )(embedded[0], norm_gain, expert_ids[0].swapaxes(1, 2), route_gates[0].swapaxes(1, 2), gate_proj[0], up_proj[0], down_proj[0])
    return out[None]


def solution(mesh):
    specs = (
        P("section", "expert", None),
        P("section", None),
        P("section", None, "expert"),
        P("section", None, "expert"),
        P("section", "expert", None),
        P("section", None, "expert", None),
        P("section", None, "expert", None),
    )
    return jax.shard_map(
        shards, mesh=mesh, in_specs=specs, out_specs=P("section", "expert", None), check_vma=False
    )
```
